128 devices in a mesh: seq: 16 (over y, z), head: 8 (over x, core).
Axes of the slice: x: 4, y: 4, z: 4, core: 2. Of those that a mesh axis runs over, the one named last changes fastest.
Arguments:
- qkv: bfloat16 [12288, 3, 3072], P(('seq', 'head')), may hold values from -21 to 21, as said below
- window_tiles: int32 [32, 27], replicated, may hold values from -1 to 31, as said below
Outputs:
- attended: bfloat16 [12288, 3072], P(('seq', 'head'))
The draws below stay inside these ranges and needn't reach their ends.
Inputs may be any that keep to these rules, and one draw needn't show every extreme that they name: `window_tiles`: row a lists distinct tile ids or -1; its first entry is a itself; every other id is of a tile that differs from tile a by at most one tile in time, in height and in width. `qkv`: entries are finite.
All inputs are finite; a program needn't handle non-finite values.
Results may differ from the reference program's by a relative error of at most 0.012.
Values may be sent and summed in bfloat16 or wider, within the bound.
A program may use at most 128 MiB of HBM per device.

```python
import jax
import jax.numpy as jnp
import numpy as np
from jax import lax

D = 3072
HEADS = 24
HDIM = 128
TF = 6
TH = 8
TW = 8
KSLOTS = 27
TT = 2
HT = 4
WT = 4
TILE = 384
TOKENS = 12288
NTILES = 32


def draw_window_tiles(key, part):
    tile_ids = jnp.arange(NTILES, dtype=jnp.int32)
    owner = tile_ids // TT
    moment = tile_ids % TT
    height = owner // WT
    column = owner % WT
    offsets = np.array([(a, b, c) for a in (-1, 0, 1) for b in (-1, 0, 1) for c in (-1, 0, 1) if (a, b, c) != (0, 0, 0)], dtype=np.int32)
    next_t = moment[:, None] + offsets[None, :, 0]
    next_h = height[:, None] + offsets[None, :, 1]
    next_w = column[:, None] + offsets[None, :, 2]
    inside = (next_t >= 0) & (next_t < TT) & (next_h >= 0) & (next_h < HT) & (next_w >= 0) & (next_w < WT)
    candidate = (next_h * WT + next_w) * TT + next_t
    first_key, second_key = jax.random.split(key)
    keeping = jax.random.randint(first_key, (NTILES, 26), 0, 4) > 0
    order = jnp.arange(26, dtype=jnp.int32)
    priority = jax.random.randint(second_key, (NTILES, 26), 0, 1 << 16) * 32 + order[None, :]
    priority = jnp.where(inside & keeping, priority, -1 - order[None, :])
    top_vals, top_idx = lax.top_k(priority, KSLOTS - 1)
    chosen = jnp.take_along_axis(candidate, top_idx, axis=1)
    chosen = jnp.where(top_vals >= 0, chosen, -1)
    return jnp.concatenate([tile_ids[:, None], chosen], axis=1).astype(jnp.int32)


def draw_qkv(key, part):
    base = jnp.clip(jax.random.normal(key, (TOKENS, 3, D), jnp.float32), -5.0, 5.0)
    return base.astype(jnp.bfloat16)


def setup_inputs(seed: int = 0) -> dict:
    streams_of = jax.random.split(jax.random.key(seed), 3)
    return {
        "qkv": draw_qkv(jax.random.fold_in(streams_of[2], 71), 0),
        "window_tiles": draw_window_tiles(jax.random.fold_in(streams_of[2], 71), 0),
    }


def reference(qkv, window_tiles):
    tiles = qkv.reshape(TT, TF, HT, TH, WT, TW, 3, D)
    tiles = tiles.transpose(2, 4, 0, 1, 3, 5, 6, 7).reshape(NTILES, TILE, 3, D)
    scale = HDIM ** -0.5

    def one_tile(args):
        query, picks = args
        usable = picks >= 0
        chosen = tiles[jnp.where(usable, picks, 0).astype(jnp.int32)]
        keys = chosen[:, :, 1].reshape(KSLOTS * TILE, HEADS, HDIM).astype(jnp.float32)
        values = chosen[:, :, 2].reshape(KSLOTS * TILE, HEADS, HDIM).astype(jnp.float32)
        queries = query.reshape(TILE, HEADS, HDIM).astype(jnp.float32)
        scores = jnp.einsum("qhd,khd->hqk", queries, keys) * scale
        usable_rows = jnp.repeat(usable, TILE)
        scores = jnp.where(usable_rows[None, None, :], scores, -1e30)
        peak = jnp.max(scores, axis=2, keepdims=True)
        expo = jnp.exp(scores - peak)
        weights = (expo / jnp.sum(expo, axis=2, keepdims=True)).astype(jnp.bfloat16)
        result = jnp.einsum("hqk,khd->qhd", weights.astype(jnp.float32), values)
        return result.astype(jnp.bfloat16).reshape(TILE, D)

    outcome = lax.map(one_tile, (tiles[:, :, 0], window_tiles))
    outcome = outcome.reshape(HT, WT, TT, TF, TH, TW, D).transpose(2, 3, 0, 4, 1, 5, 6)
    return outcome.reshape(TOKENS, D)
```

```python
import jax
import jax.numpy as jnp
from jax import lax
from jax.experimental import pallas as pl
from jax.experimental.pallas import tpu as pltpu
from jax.sharding import PartitionSpec as P

HEADS = 24
HDIM = 128
TF = 6
TH = 8
TW = 8
HT = 4
WT = 4
TILE = TF * TH * TW
LINES = 3
ROWS = LINES * TW
PEERS = 64
OWNERS = 48
KCOLS = 3
QCOLS = 2
SLOTS = 27
MESH = pl.DeviceIdType.MESH
SCALE = HDIM**-0.5
LOG2E = 1.4426950408889634


def place():
    seq = lax.axis_index("seq")
    head = lax.axis_index("head")
    rank = lax.rem(head // 2 + seq // 4 + lax.rem(seq, 4), 4)
    return seq, head, rank, lax.rem(head, 2)


def bring(packed, queries, keyvals, send_q, recv_q, send_kv, recv_kv, send_x, recv_x):
    seq, head, rank, core = place()
    time = seq // 8
    mine = lax.rem(seq, 8) * 8 + head
    owner = rank < 3
    to_self = owner & (core == time)

    def copies(step):
        there = lax.rem(seq + step, 16)
        row = lax.rem(step // 16 + seq, 3)
        half = lax.rem(there, 2)
        which = row * 8 + there // 2
        chip = lax.rem(row + 8 - there // 4 - lax.rem(there, 4), 4)
        target = chip * 2 + time
        pairs = (
            (packed.at[0, pl.ds(2 * half, QCOLS), which], queries.at[:, mine], send_q, recv_q),
            (packed.at[pl.ds(1, 2), pl.ds(half, KCOLS), which], keyvals.at[time, :, :, mine], send_kv, recv_kv),
        )
        return there, target, pairs

    def start(step, carry):
        there, target, pairs = copies(step)
        own = (there == seq) & (target == head)

        @pl.when(own)
        def _():
            for source, landing, _, arrived in pairs:
                pltpu.make_async_copy(source, landing, arrived).start()

        @pl.when(jnp.logical_not(own))
        def _():
            for source, landing, sent, arrived in pairs:
                pltpu.make_async_remote_copy(
                    src_ref=source,
                    dst_ref=landing,
                    send_sem=sent,
                    recv_sem=arrived,
                    device_id=(there, target),
                    device_id_type=MESH,
                ).start()

        return carry

    lax.fori_loop(0, OWNERS, start, 0)

    @pl.when(owner)
    def _():
        pltpu.make_async_copy(keyvals.at[core], keyvals.at[core], recv_kv).wait()
        swap = pltpu.make_async_remote_copy(
            src_ref=keyvals.at[core],
            dst_ref=keyvals.at[core],
            send_sem=send_x,
            recv_sem=recv_x,
            device_id=(seq, head + 1 - 2 * core),
            device_id_type=MESH,
        )
        swap.start()
        pltpu.make_async_copy(queries, queries, recv_q).wait()
        swap.wait_send()
        pltpu.make_async_copy(keyvals.at[1 - core], keyvals.at[1 - core], recv_x).wait()

    def sent(count):
        spread = keyvals.at[0, :, :, pl.ds(0, count)]
        pltpu.make_async_copy(spread, spread, send_kv).wait()
        spread = queries.at[:, pl.ds(0, count)]
        pltpu.make_async_copy(spread, spread, send_q).wait()

    @pl.when(to_self)
    def _():
        sent(OWNERS - 1)

    @pl.when(jnp.logical_not(to_self))
    def _():
        sent(OWNERS)


def attend(meta, table, q_ref, kv_ref, o_ref, top, total, acc):
    column, band = pl.program_id(0), pl.program_id(1)
    half, time, owner = meta[0], meta[1], meta[2]
    here = (band * WT + 2 * half + column) * 2 + time

    @pl.when(owner == 1)
    def _():
        query = q_ref[0, :, 0].reshape(TILE, HDIM)
        top[...] = jnp.full_like(top, -jnp.inf)
        total[...] = jnp.zeros_like(total)
        acc[...] = jnp.zeros_like(acc)

        def slot(index, carry):
            pick = table[here, index]

            @pl.when(pick >= 0)
            def _():
                moment = lax.rem(pick, 2)
                across = lax.rem(pick // 2, WT) - half
                down = pick // (2 * WT)
                keys = kv_ref[moment, 0, across, :, down].reshape(TILE, HDIM)
                values = kv_ref[moment, 1, across, :, down].reshape(TILE, HDIM)
                scores = lax.dot_general(query, keys, (((1,), (1,)), ((), ())), preferred_element_type=jnp.float32)
                before = top[...]
                peak = jnp.maximum(before, jnp.max(scores, axis=1, keepdims=True))
                top[...] = peak
                fade = jnp.exp2((before - peak) * (SCALE * LOG2E))
                expo = jnp.exp2((scores - peak[:, :1]) * (SCALE * LOG2E))
                lanes = expo[:, :HDIM] + expo[:, HDIM : 2 * HDIM] + expo[:, 2 * HDIM :]
                total[...] = total[...] * fade + lanes
                acc[...] = acc[...] * fade + jnp.dot(
                    expo.astype(jnp.bfloat16), values, preferred_element_type=jnp.float32
                )

            return carry

        lax.fori_loop(0, SLOTS, slot, 0)
        denominator = jnp.sum(total[...], axis=1, keepdims=True)
        o_ref[0, :, 0] = (acc[...] / denominator).astype(jnp.bfloat16).reshape(TF, TH * TW, HDIM)


def give(answers, stage, send, recv):
    seq, head, rank, core = place()
    owner = rank < 3
    to_self = owner & (core == seq // 8)
    which = rank * 8 + seq // 2
    half = lax.rem(seq, 2)

    @pl.when(owner)
    def _():
        def start(step, carry):
            number = lax.rem(step + lax.rem(seq, 8) * 8 + head, PEERS)
            there = core * 8 + number // 8
            target = lax.rem(number, 8)
            source = answers.at[:, number]
            landing = stage.at[pl.ds(2 * half, QCOLS), which]
            own = (there == seq) & (target == head)

            @pl.when(own)
            def _():
                pltpu.make_async_copy(source, landing, recv).start()

            @pl.when(jnp.logical_not(own))
            def _():
                pltpu.make_async_remote_copy(
                    src_ref=source,
                    dst_ref=landing,
                    send_sem=send,
                    recv_sem=recv,
                    device_id=(there, target),
                    device_id_type=MESH,
                ).start()

            return carry

        lax.fori_loop(0, PEERS, start, 0)

    pltpu.make_async_copy(stage, stage, recv).wait()

    def sent(count):
        spread = answers.at[:, pl.ds(0, count)]
        pltpu.make_async_copy(spread, spread, send).wait()

    @pl.when(to_self)
    def _():
        sent(PEERS - 1)

    @pl.when(owner & jnp.logical_not(to_self))
    def _():
        sent(PEERS)


def body(qkv, window_tiles):
    seq, _, rank, core = place()
    anywhere = pl.BlockSpec(memory_space=pl.ANY)
    packed = qkv.reshape(LINES, WT, TW, 3, HEADS, HDIM).transpose(3, 1, 4, 0, 2, 5).reshape(3, WT, HEADS, ROWS, HDIM)
    queries, keyvals = pl.pallas_call(
        bring,
        out_shape=(
            jax.ShapeDtypeStruct((QCOLS, PEERS, ROWS, HDIM), jnp.bfloat16),
            jax.ShapeDtypeStruct((2, 2, KCOLS, PEERS, ROWS, HDIM), jnp.bfloat16),
        ),
        in_specs=[anywhere],
        out_specs=(anywhere, anywhere),
        scratch_shapes=[pltpu.SemaphoreType.DMA] * 6,
        compiler_params=pltpu.CompilerParams(has_side_effects=True),
        name="bring",
    )(packed)
    meta = jnp.stack([lax.rem(seq, 2), core, (rank < 3).astype(jnp.int32)])
    answers = pl.pallas_call(
        attend,
        out_shape=jax.ShapeDtypeStruct((QCOLS, TF, HT, TH * TW, HDIM), jnp.bfloat16),
        grid_spec=pltpu.PrefetchScalarGridSpec(
            num_scalar_prefetch=2,
            grid=(QCOLS, HT),
            in_specs=[
                pl.BlockSpec((1, TF, 1, TH * TW, HDIM), lambda i, j, *_: (i, 0, j, 0, 0)),
                pl.BlockSpec(memory_space=pltpu.VMEM),
            ],
            out_specs=pl.BlockSpec((1, TF, 1, TH * TW, HDIM), lambda i, j, *_: (i, 0, j, 0, 0)),
            scratch_shapes=[pltpu.VMEM((TILE, HDIM), jnp.float32)] * 3,
        ),
        compiler_params=pltpu.CompilerParams(vmem_limit_bytes=40 << 20),
        name="attend",
    )(
        meta,
        window_tiles,
        queries.reshape(QCOLS, TF, HT, TH * TW, HDIM),
        keyvals.reshape(2, 2, KCOLS, TF, HT, TH * TW, HDIM),
    )
    stage = pl.pallas_call(
        give,
        out_shape=jax.ShapeDtypeStruct((WT, HEADS, ROWS, HDIM), jnp.bfloat16),
        in_specs=[anywhere],
        out_specs=anywhere,
        scratch_shapes=[pltpu.SemaphoreType.DMA] * 2,
        compiler_params=pltpu.CompilerParams(has_side_effects=True),
        name="give",
    )(answers.reshape(QCOLS, PEERS, ROWS, HDIM))
    return stage.reshape(WT, HEADS, LINES, TW, HDIM).transpose(2, 0, 3, 1, 4).reshape(LINES * WT * TW, HEADS * HDIM)


def solution(mesh):
    in_specs = (P(("seq", "head"), None, None), P())
    out_specs = P(("seq", "head"), None)
    return jax.shard_map(body, mesh=mesh, in_specs=in_specs, out_specs=out_specs, check_vma=False)
```
